32 devices in a mesh: seq: 16 (over z, y, x), head: 2 (over core).
Axes of the slice: x: 2, y: 2, z: 4, core: 2. Of those that a mesh axis runs over, the one named last changes fastest.
Arguments:
- queries: bfloat16 [2048, 32, 128], P('seq', 'head'), may hold values from -6 to 6
- key_vectors: bfloat16 [2048, 32, 128], P('seq', 'head'), may hold values from -6 to 6
- values: bfloat16 [2048, 32, 128], P('seq', 'head'), may hold values from -6 to 6
- out_grad: bfloat16 [2048, 32, 128], P('seq', 'head'), may hold values from -6 to 6
- hidden_in: bfloat16 [2048, 2048], P('seq'), may hold values from -6 to 6
- decay_weight: bfloat16 [2048, 32], P(None, 'head'), may hold values from -0.125 to 0.125
- write_weight: bfloat16 [2048, 32], P(None, 'head'), may hold values from -0.125 to 0.125
- decay_bias: float32 [32], P('head'), may hold values from -2 to 2
- decay_log: float32 [32], P('head'), may hold values from -11 to -2
- write_bias: float32 [32], P('head'), may hold values from -9 to 0
- start_state: float32 [16, 32, 128, 128], P('seq', 'head'), may hold values from -4 to 4
Outputs:
- grad_queries: bfloat16 [2048, 32, 128], P('seq', 'head')
- grad_keys: bfloat16 [2048, 32, 128], P('seq', 'head')
- grad_values: bfloat16 [2048, 32, 128], P('seq', 'head')
- grad_hidden: bfloat16 [2048, 2048], P('seq', 'head')
- grad_decay_weight: float32 [2048, 32], P(None, 'head')
- grad_write_weight: float32 [2048, 32], P(None, 'head')
The draws below stay inside these ranges and needn't reach their ends.
All inputs are finite; a program needn't handle non-finite values.
Results may differ from the reference program's by a relative error of at most 0.014.
Values may be sent and summed in bfloat16 or wider, within the bound.
A program may use at most 128 MiB of HBM per device.

```python
from functools import partial
import jax
import jax.numpy as jnp
from jax import lax

D = 2048
HEADS = 32
DK = 128
DV = 128
TOK_DEV = 128
BLOCKS = 16
TOKENS = 2048


def block_scale(own_key, extent, shards, least, top_value):
    def one(axis_at, blocks):
        draws = jax.random.uniform(jax.random.fold_in(jax.random.fold_in(own_key, 6), axis_at), (blocks,), jnp.float32, least / len(shards), top_value / len(shards))
        return jnp.repeat(jnp.exp(draws), extent[axis_at] // blocks).reshape((-1,) + (1,) * (len(extent) - axis_at - 1))

    level = one(*shards[0])
    for cut in shards[1:]:
        level = level * one(*cut)
    return level


def scatter_about(own_key, extent, scale, most, split=(), held_as=jnp.bfloat16):
    loudness = block_scale(own_key, extent, split, -0.22, 0.18) if split else 1.0
    array = jax.random.normal(own_key, extent, jnp.float32) * scale * loudness
    return jnp.minimum(jnp.maximum(array, -most), most).astype(held_as)


def setup_inputs(seed: int = 0) -> dict:
    key_of = jax.random.split(jax.random.key(seed), 12)
    return {
        "queries": scatter_about(key_of[0], (TOKENS, HEADS, DK), 1.0, 6.0, ((0, 16), (1, 2))),
        "key_vectors": scatter_about(key_of[1], (TOKENS, HEADS, DK), 1.0, 6.0, ((0, 16), (1, 2))),
        "values": scatter_about(key_of[2], (TOKENS, HEADS, DV), 1.0, 6.0, ((0, 16), (1, 2))),
        "out_grad": scatter_about(key_of[3], (TOKENS, HEADS, DV), 1.0, 6.0, ((0, 16), (1, 2))),
        "hidden_in": scatter_about(key_of[4], (TOKENS, D), 1.0, 6.0, ((0, 16),)),
        "decay_weight": scatter_about(key_of[5], (D, HEADS), D ** -0.5, 0.125, ((1, 2),)),
        "write_weight": scatter_about(key_of[6], (D, HEADS), D ** -0.5, 0.125, ((1, 2),)),
        "decay_bias": jnp.clip(jax.random.uniform(key_of[7], (HEADS,), jnp.float32, -2.0, 2.0) * block_scale(key_of[7], (HEADS,), ((0, 2),), -0.4, 0.0), -2.0, 2.0),
        "decay_log": jnp.clip(-11.0 + 9.0 * jax.random.uniform(key_of[8], (HEADS,), jnp.float32) ** block_scale(key_of[8], (HEADS,), ((0, 2),), -0.2, 0.2), -11.0, -2.0),
        "write_bias": jnp.clip(-9.0 + 9.0 * jax.random.uniform(key_of[9], (HEADS,), jnp.float32) ** block_scale(key_of[9], (HEADS,), ((0, 2),), -0.2, 0.2), -9.0, 0.0),
        "start_state": scatter_about(key_of[10], (BLOCKS, HEADS, DK, DV), 0.5, 4.0, ((0, 16), (1, 2)), jnp.float32),
    }


EPSILON = 1e-06
PRECISION_MAXIMUM = lax.Precision.HIGHEST

def block_forward(decay_log, decay_bias, write_bias, queries, key_vectors, values, decay_logit, write_logit, initial_state):
    normalized_queries = queries * lax.rsqrt(lax.optimization_barrier(jnp.sum(queries * queries, axis=-1, keepdims=True)) + EPSILON)
    normalized_keys = key_vectors * lax.rsqrt(lax.optimization_barrier(jnp.sum(key_vectors * key_vectors, axis=-1, keepdims=True)) + EPSILON)
    write_rate = jax.nn.sigmoid(write_logit + write_bias)
    log_decay = -jnp.exp(decay_log) * jax.nn.softplus(decay_logit + decay_bias)
    log_prefix = jnp.cumsum(log_decay, axis=0).T
    block_size = queries.shape[0]
    positions = jnp.arange(block_size, dtype=jnp.int32)
    lower_mask = positions[:, None] >= positions[None, :]
    strict_mask = positions[:, None] > positions[None, :]
    log_gaps = jnp.where(lower_mask, log_prefix[:, :, None] - log_prefix[:, None, :], 0.0)
    decay_ratio = jnp.where(lower_mask, jnp.exp(log_gaps), 0.0)
    key_gram = jnp.einsum('ihk,jhk->hij', normalized_keys, normalized_keys, precision=PRECISION_MAXIMUM)
    coupling = jnp.where(strict_mask, write_rate.T[:, :, None] * decay_ratio * key_gram, 0.0)
    unit_lower = coupling + jnp.eye(block_size, dtype=coupling.dtype)
    cumulative_decay = jnp.exp(log_prefix)
    keys_against_state = jnp.einsum('dlu,lux->ldx', normalized_keys, initial_state, precision=PRECISION_MAXIMUM)
    right_side = write_rate.T[:, :, None] * (jnp.swapaxes(values, 0, 1) - cumulative_decay[:, :, None] * keys_against_state)
    value_updates = jax.scipy.linalg.solve_triangular(unit_lower, right_side, lower=True, unit_diagonal=True)
    query_keys = decay_ratio * jnp.einsum('ihk,jhk->hij', normalized_queries, normalized_keys, precision=PRECISION_MAXIMUM)
    layer_outputs = cumulative_decay[:, :, None] * jnp.einsum('dlu,lux->ldx', normalized_queries, initial_state, precision=PRECISION_MAXIMUM)
    layer_outputs = layer_outputs + jnp.einsum('hij,hjv->hiv', query_keys, value_updates, precision=PRECISION_MAXIMUM)
    final_decay_weights = decay_ratio[:, -1, :]
    final_state = cumulative_decay[:, -1][:, None, None] * initial_state + jnp.einsum('zg,gzi,zgq->ziq', final_decay_weights, normalized_keys, value_updates, precision=PRECISION_MAXIMUM)
    return (jnp.swapaxes(layer_outputs, 0, 1), final_state)

def reference(queries, key_vectors, values, out_grad, hidden_in, decay_weight, write_weight, decay_bias, decay_log, write_bias, start_state):
    decay_logit = jnp.dot(hidden_in.astype(jnp.float32), decay_weight.astype(jnp.float32), preferred_element_type=jnp.float32)
    write_logit = jnp.dot(hidden_in.astype(jnp.float32), write_weight.astype(jnp.float32), preferred_element_type=jnp.float32)
    head_count = queries.shape[1]

    def blocked(source):
        return source.astype(jnp.float32).reshape((BLOCKS, TOK_DEV) + source.shape[1:])
    inputs = (blocked(queries), blocked(key_vectors), blocked(values), blocked(out_grad), blocked(decay_logit), blocked(write_logit), start_state)
    forward = partial(block_forward, decay_log, decay_bias, write_bias)

    def backward_block(carried, pieces):
        query_rows, key_rows, value_rows, grad_rows, decay_rows, write_rows, initial_state = pieces
        primal, pullback = jax.vjp(forward, query_rows, key_rows, value_rows, decay_rows, write_rows, initial_state)
        gradients = pullback((grad_rows, carried))
        return (gradients[5], gradients[:5])
    carried_init = jnp.zeros((head_count, DK, DV), jnp.float32)
    _, gradients = lax.scan(backward_block, carried_init, inputs, reverse=True)

    def joined(source):
        return source.reshape((TOKENS,) + source.shape[2:])
    grad_queries = joined(gradients[0]).astype(jnp.bfloat16)
    grad_keys = joined(gradients[1]).astype(jnp.bfloat16)
    grad_values = joined(gradients[2]).astype(jnp.bfloat16)
    decay_grads = joined(gradients[3]).astype(jnp.bfloat16)
    write_grads = joined(gradients[4]).astype(jnp.bfloat16)
    grad_decay_weight = jnp.dot(hidden_in.T.astype(jnp.float32), decay_grads.astype(jnp.float32), preferred_element_type=jnp.float32)
    grad_write_weight = jnp.dot(hidden_in.T.astype(jnp.float32), write_grads.astype(jnp.float32), preferred_element_type=jnp.float32)
    grad_hidden = jnp.dot(decay_grads.astype(jnp.float32), decay_weight.T.astype(jnp.float32), preferred_element_type=jnp.float32) + jnp.dot(write_grads.astype(jnp.float32), write_weight.T.astype(jnp.float32), preferred_element_type=jnp.float32)
    return (grad_queries, grad_keys, grad_values, grad_hidden.astype(jnp.bfloat16), grad_decay_weight, grad_write_weight)
```

```python
from functools import partial

import jax
import jax.numpy as jnp
from jax import lax
from jax.experimental import pallas as pl
from jax.experimental.pallas import tpu as pltpu
from jax.sharding import PartitionSpec as P

EPSILON = 1e-06
HI = lax.Precision.HIGHEST
F32 = jnp.float32
BF = jnp.bfloat16


def mm(a, b, ca=1, cb=0):
    return lax.dot_general(
        a.astype(BF), b.astype(BF), (((ca,), (cb,)), ((), ())), preferred_element_type=F32
    )


def unit(x):
    r = lax.rsqrt(jnp.sum(x * x, axis=1, keepdims=True) + EPSILON)
    return x * r, r


def unit_back(d, n, r):
    return r * (d - n * jnp.sum(n * d, axis=1, keepdims=True))


def indices(c):
    row = lax.broadcasted_iota(jnp.int32, (c, c), 0)
    col = lax.broadcasted_iota(jnp.int32, (c, c), 1)
    return row, col


def local_head(q, k, v, do, s0, rows):
    c = q.shape[0]
    row, col = indices(c)
    cols = rows.T
    g_col, beta = cols[:, 0:1], cols[:, 1:2]
    g_row = rows[0:1, :]
    g_last = g_row[:, c - 1 : c]
    cd = jnp.exp(g_col)
    to_end = jnp.exp(g_last - g_col)
    lower = row >= col
    gamma = jnp.where(lower, jnp.exp(jnp.where(lower, g_col - g_row, 0.0)), 0.0)
    gamma_strict = jnp.where(row > col, gamma, 0.0)
    qn, rq = unit(q.astype(F32))
    kn, _ = unit(k.astype(F32))
    qb, kb, sb = qn.astype(BF), kn.astype(BF), s0.astype(BF)
    gram = gamma_strict * mm(kb, kb, 1, 1)
    p = gamma * mm(qb, kb, 1, 1)
    z = v.astype(F32) - cd * mm(kb, sb)
    a = beta * gram
    inv = jnp.where(row == col, 1.0, jnp.where((row ^ col) == 1, -a, 0.0))
    level = 1
    while (2 << level) <= c:
        low, high = row >> level, col >> level
        band = jnp.where(((low ^ high) == 1), a, 0.0)
        inv = inv - mm(mm(inv, band), inv)
        level += 1
    ib = inv.astype(BF)
    ub = mm(ib, beta * z).astype(BF)
    ptdo = mm(p, do, 0, 0)
    w0 = mm(ib, ptdo, 0, 0)
    nb = mm(ib, to_end * kn, 0, 0).astype(BF)
    bck = ((beta * cd) * kn).astype(BF)
    off = mm(cd * qn, do, 0, 0) - mm(bck, w0, 0, 0)
    tt = mm(bck, nb, 0, 0)
    dp = mm(do, ub, 1, 1)
    dos = cd * mm(do, sb, 1, 1)
    gdp = (gamma * dp).astype(BF)
    dq = unit_back(dos + mm(gdp, kb), qn, rq)
    dk0 = mm(gdp, qb, 0, 0)
    t = dp * p
    dg0 = jnp.sum((t + dos * qn).T, axis=0, keepdims=True) - jnp.sum(t, axis=0, keepdims=True)
    return dq, ub, w0, nb, tt, off, z, gram, gamma_strict, dk0, dg0


def carry_head(k, v, s0, e, rows, ub, w0, nb, z, gram, gamma_strict, dk0, dg0):
    c = k.shape[0]
    row, col = indices(c)
    cols = rows.T
    g_col, beta = cols[:, 0:1], cols[:, 1:2]
    g_last = rows[0:1, c - 1 : c]
    cd = jnp.exp(g_col)
    to_end = jnp.exp(g_last - g_col)
    kn, rk = unit(k.astype(F32))
    kb = kn.astype(BF)
    w = w0 + mm(nb, e)
    wb = w.astype(BF)
    dv = beta * w
    da = -mm(wb, ub, 1, 1)
    ws = mm(wb, s0, 1, 1)
    ue = to_end * mm(ub, e, 1, 1)
    dkk = (beta * gamma_strict * da).astype(BF)
    dkn = dk0 - (beta * cd) * ws + mm(dkk, kb) + mm(dkk, kb, 0, 0) + ue
    dk = unit_back(dkn, kn, rk)
    dagram = da * gram
    t = beta * dagram
    s = kn * ue
    dbeta = jnp.sum((dagram + w * z).T, axis=0, keepdims=True)
    dg = dg0 - jnp.sum(t, axis=0, keepdims=True)
    dg = dg + jnp.sum((t - dv * (v.astype(F32) - z) - s).T, axis=0, keepdims=True)
    tail = jnp.sum(s, keepdims=True) + jnp.exp(g_last) * jnp.sum(s0 * e.astype(F32), keepdims=True)
    lane = lax.broadcasted_iota(jnp.int32, (1, c), 1)
    dg = dg + jnp.where(lane == c - 1, tail, 0.0)
    return dv, dk, dg, dbeta


def local_kernel(q, k, v, do, s0, rows, dq, ub, w0, nb, tt, off, z, gram, gs, dk0, dg0):
    for i in range(q.shape[0]):
        outs = local_head(q[i], k[i], v[i], do[i], s0[i], rows[i])
        for ref, value in zip((dq, ub, w0, nb, tt, off, z, gram, gs, dk0, dg0), outs):
            ref[i] = value.astype(ref.dtype)


def carry_kernel(k, v, s0, e, rows, ub, w0, nb, z, gram, gs, dk0, dg0, dv, dk, dg, dbeta):
    for i in range(k.shape[0]):
        outs = carry_head(
            k[i], v[i], s0[i], e[i], rows[i], ub[i], w0[i], nb[i], z[i], gram[i], gs[i], dk0[i], dg0[i]
        )
        for ref, value in zip((dv, dk, dg, dbeta), outs):
            ref[i] = value.astype(ref.dtype)


def chain_kernel(n, tt, off, rows, e_out, inbuf, outbuf, send_sem, recv_sem):
    me = lax.axis_index("seq")
    heads, c = tt.shape[0], rows.shape[2]
    barrier = pltpu.get_barrier_semaphore()
    mesh_id = pl.DeviceIdType.MESH

    @pl.when(me > 0)
    def _():
        pl.semaphore_signal(barrier, inc=1, device_id={"seq": me - 1}, device_id_type=mesh_id)

    @pl.when(me < n - 1)
    def _():
        pl.semaphore_signal(barrier, inc=1, device_id={"seq": me + 1}, device_id_type=mesh_id)

    peers = jnp.where(me > 0, 1, 0) + jnp.where(me < n - 1, 1, 0)
    pl.semaphore_wait(barrier, peers)

    def copy(h):
        return pltpu.make_async_remote_copy(
            src_ref=outbuf.at[h],
            dst_ref=inbuf.at[h],
            send_sem=send_sem.at[h],
            recv_sem=recv_sem.at[h],
            device_id={"seq": me - 1},
            device_id_type=mesh_id,
        )

    @pl.when(me == n - 1)
    def _():
        def first(h, _):
            outbuf[h] = off[h].astype(BF)
            copy(h).start()
            e_out[h] = jnp.zeros(e_out.shape[1:], e_out.dtype)
            return 0

        lax.fori_loop(0, heads, first, 0)

    @pl.when(me < n - 1)
    def _():
        def step(h, _):
            copy(h).wait_recv()
            e = inbuf[h]
            e_out[h] = e

            @pl.when(me > 0)
            def _():
                cdl = jnp.exp(rows[h, 0:1, c - 1 : c])
                outbuf[h] = (off[h] + cdl * e.astype(F32) - mm(tt[h], e)).astype(BF)
                copy(h).start()

            return 0

        lax.fori_loop(0, heads, step, 0)

    @pl.when(me > 0)
    def _():
        def done(h, _):
            copy(h).wait_send()
            return 0

        lax.fori_loop(0, heads, done, 0)


def per_head(kernel, group, ins, outs):
    heads = ins[0].shape[0]

    def spec(a):
        return pl.BlockSpec((group,) + a.shape[1:], lambda h: (h, 0, 0))

    return pl.pallas_call(
        kernel,
        grid=(heads // group,),
        out_shape=outs,
        in_specs=[spec(a) for a in ins],
        out_specs=[spec(a) for a in outs],
        compiler_params=pltpu.CompilerParams(vmem_limit_bytes=48 * 1024 * 1024),
    )(*ins)


def local_part(q, k, v, do, s0, rows):
    h, c, dk = q.shape
    dv = v.shape[2]
    sd = jax.ShapeDtypeStruct
    outs = [
        sd((h, c, dk), BF), sd((h, c, dv), BF), sd((h, c, dv), F32), sd((h, c, dk), BF),
        sd((h, dk, dk), BF), sd((h, dk, dv), F32), sd((h, c, dv), F32), sd((h, c, c), F32),
        sd((h, c, c), F32), sd((h, c, dk), F32), sd((h, 1, c), F32),
    ]
    return per_head(local_kernel, 4, (q, k, v, do, s0, rows), outs)


def carry_part(k, v, s0, e, rows, saved):
    h, c, dk = k.shape
    dv = v.shape[2]
    sd = jax.ShapeDtypeStruct
    outs = [sd((h, c, dv), BF), sd((h, c, dk), BF), sd((h, 1, c), F32), sd((h, 1, c), F32)]
    return per_head(carry_kernel, 4, (k, v, s0, e, rows) + saved, outs)


def chain_part(n, tt, off, rows):
    vm = pl.BlockSpec(memory_space=pltpu.VMEM)
    h = tt.shape[0]
    return pl.pallas_call(
        partial(chain_kernel, n),
        out_shape=jax.ShapeDtypeStruct(off.shape, BF),
        in_specs=[vm] * 3,
        out_specs=vm,
        scratch_shapes=[
            pltpu.VMEM(off.shape, BF),
            pltpu.VMEM(off.shape, BF),
            pltpu.SemaphoreType.DMA((h,)),
            pltpu.SemaphoreType.DMA((h,)),
        ],
        compiler_params=pltpu.CompilerParams(collective_id=0, has_side_effects=True),
    )(tt, off, rows)


def gates(hidden_in, both, decay_bias, decay_log, write_bias):
    h = decay_bias.shape[0]
    logits = lax.dot_general(
        both, hidden_in, (((0,), (1,)), ((), ())), preferred_element_type=F32
    )
    pre = logits[:h] + decay_bias[:, None]
    rate = jnp.exp(decay_log)[:, None]
    beta = jax.nn.sigmoid(logits[h:] + write_bias[:, None])
    log_decay = -rate * jax.nn.softplus(pre)
    c = log_decay.shape[1]
    ones = jnp.triu(jnp.ones((c, c), F32))
    g = jnp.dot(log_decay, ones, precision=HI)
    return pre, rate, beta, g, ones


def shards(
    queries,
    key_vectors,
    values,
    out_grad,
    hidden_in,
    decay_weight,
    write_weight,
    decay_bias,
    decay_log,
    write_bias,
    start_state,
):
    n = lax.axis_size("seq")
    both = jnp.concatenate([decay_weight, write_weight], axis=1)
    pre, rate, beta, g, ones = gates(hidden_in, both, decay_bias, decay_log, write_bias)
    h, c = g.shape
    rows = jnp.concatenate(
        [g[:, None], beta[:, None], jnp.zeros((h, 6, c), F32)], axis=1
    )
    q, k, v, do = (jnp.swapaxes(a, 0, 1) for a in (queries, key_vectors, values, out_grad))
    s0 = start_state[0]
    dq, ub, w0, nb, tt, off, z, gram, gs, dk0, dg0 = local_part(q, k, v, do, s0, rows)
    e = chain_part(n, tt, off, rows)
    dv, dk, dg, dbeta = carry_part(k, v, s0, e, rows, (ub, w0, nb, z, gram, gs, dk0, dg0))
    dlog = jnp.dot(dg[:, 0], ones.T, precision=HI)
    decay_grads = (-dlog * rate * jax.nn.sigmoid(pre)).astype(BF)
    write_grads = (dbeta[:, 0] * beta * (1.0 - beta)).astype(BF)
    grads = jnp.concatenate([decay_grads, write_grads], axis=0)
    weight_terms = jnp.dot(grads, hidden_in, preferred_element_type=F32)
    total = lax.psum(weight_terms, "seq")
    partial_terms = lax.dot_general(
        grads, both, (((0,), (1,)), ((), ())), preferred_element_type=F32
    )
    grad_hidden = lax.psum_scatter(
        partial_terms.astype(BF), "head", scatter_dimension=1, tiled=True
    )
    return (
        jnp.swapaxes(dq, 0, 1),
        jnp.swapaxes(dk, 0, 1),
        jnp.swapaxes(dv, 0, 1),
        grad_hidden,
        total[:h].T,
        total[h:].T,
    )


def solution(mesh):
    placed = (
        P("seq", "head", None),
        P("seq", "head", None),
        P("seq", "head", None),
        P("seq", "head", None),
        P("seq", None),
        P(None, "head"),
        P(None, "head"),
        P("head"),
        P("head"),
        P("head"),
        P("seq", "head", None, None),
    )
    return jax.shard_map(
        shards,
        mesh=mesh,
        in_specs=placed,
        out_specs=(
            P("seq", "head", None),
            P("seq", "head", None),
            P("seq", "head", None),
            P("seq", "head"),
            P(None, "head"),
            P(None, "head"),
        ),
        check_vma=False,
    )
```

```python
from functools import partial

import jax
import jax.numpy as jnp
from jax import lax
from jax.experimental import pallas as pl
from jax.experimental.pallas import tpu as pltpu
from jax.sharding import PartitionSpec as P

EPSILON = 1e-06
HI = lax.Precision.HIGHEST
F32 = jnp.float32
BF = jnp.bfloat16


def mm(a, b, ca=1, cb=0):
    return lax.dot_general(
        a.astype(BF), b.astype(BF), (((ca,), (cb,)), ((), ())), preferred_element_type=F32
    )


def unit(x):
    r = lax.rsqrt(jnp.sum(x * x, axis=1, keepdims=True) + EPSILON)
    return x * r, r


def unit_back(d, n, r):
    return r * (d - n * jnp.sum(n * d, axis=1, keepdims=True))


def indices(c):
    row = lax.broadcasted_iota(jnp.int32, (c, c), 0)
    col = lax.broadcasted_iota(jnp.int32, (c, c), 1)
    return row, col


def local_first(q, k, v, s0, rows):
    c = q.shape[0]
    row, col = indices(c)
    cols = rows.T
    g_col, beta = cols[:, 0:1], cols[:, 1:2]
    g_row = rows[0:1, :]
    g_last = g_row[:, c - 1 : c]
    cd = jnp.exp(g_col)
    to_end = jnp.exp(g_last - g_col)
    lower = row >= col
    gamma = jnp.where(lower, jnp.exp(jnp.where(lower, g_col - g_row, 0.0)), 0.0)
    gamma_strict = jnp.where(row > col, gamma, 0.0)
    qn, rq = unit(q.astype(F32))
    kn, _ = unit(k.astype(F32))
    qb, kb, sb = qn.astype(BF), kn.astype(BF), s0.astype(BF)
    gram = gamma_strict * mm(kb, kb, 1, 1)
    p = gamma * mm(qb, kb, 1, 1)
    z = v.astype(F32) - cd * mm(kb, sb)
    a = beta * gram
    return qn, rq, qb, kn, kb, sb, p, z, a, gram, gamma, gamma_strict, beta, cd, to_end


def inverses(couplings):
    c = couplings[0].shape[0]
    row, col = indices(c)
    invs = [
        jnp.where(row == col, 1.0, jnp.where((row ^ col) == 1, -a, 0.0)) for a in couplings
    ]
    level = 1
    while (2 << level) <= c:
        near = ((row >> level) ^ (col >> level)) == 1
        halves = [mm(x, jnp.where(near, a, 0.0)) for x, a in zip(invs, couplings)]
        invs = [x - mm(y, x) for x, y in zip(invs, halves)]
        level += 1
    return invs


def local_rest(do, inv, first):
    qn, rq, qb, kn, kb, sb, p, z, a, gram, gamma, gamma_strict, beta, cd, to_end = first
    ib = inv.astype(BF)
    ub = mm(ib, beta * z).astype(BF)
    ptdo = mm(p, do, 0, 0)
    w0 = mm(ib, ptdo, 0, 0)
    nb = mm(ib, to_end * kn, 0, 0).astype(BF)
    bck = ((beta * cd) * kn).astype(BF)
    off = mm(cd * qn, do, 0, 0) - mm(bck, w0, 0, 0)
    tt = mm(bck, nb, 0, 0)
    dp = mm(do, ub, 1, 1)
    dos = cd * mm(do, sb, 1, 1)
    gdp = (gamma * dp).astype(BF)
    dq = unit_back(dos + mm(gdp, kb), qn, rq)
    dk0 = mm(gdp, qb, 0, 0)
    t = dp * p
    dg0 = jnp.sum((t + dos * qn).T, axis=0, keepdims=True) - jnp.sum(t, axis=0, keepdims=True)
    return dq, ub, w0, nb, tt, off, z, gram, gamma_strict, dk0, dg0


def carry_head(k, v, s0, e, rows, ub, w0, nb, z, gram, gamma_strict, dk0, dg0):
    c = k.shape[0]
    row, col = indices(c)
    cols = rows.T
    g_col, beta = cols[:, 0:1], cols[:, 1:2]
    g_last = rows[0:1, c - 1 : c]
    cd = jnp.exp(g_col)
    to_end = jnp.exp(g_last - g_col)
    kn, rk = unit(k.astype(F32))
    kb = kn.astype(BF)
    w = w0 + mm(nb, e)
    wb = w.astype(BF)
    dv = beta * w
    da = -mm(wb, ub, 1, 1)
    ws = mm(wb, s0, 1, 1)
    ue = to_end * mm(ub, e, 1, 1)
    dkk = (beta * gamma_strict * da).astype(BF)
    dkn = dk0 - (beta * cd) * ws + mm(dkk, kb) + mm(dkk, kb, 0, 0) + ue
    dk = unit_back(dkn, kn, rk)
    dagram = da * gram
    t = beta * dagram
    s = kn * ue
    dbeta = jnp.sum((dagram + w * z).T, axis=0, keepdims=True)
    dg = dg0 - jnp.sum(t, axis=0, keepdims=True)
    dg = dg + jnp.sum((t - dv * (v.astype(F32) - z) - s).T, axis=0, keepdims=True)
    tail = jnp.sum(s, keepdims=True) + jnp.exp(g_last) * jnp.sum(s0 * e.astype(F32), keepdims=True)
    lane = lax.broadcasted_iota(jnp.int32, (1, c), 1)
    dg = dg + jnp.where(lane == c - 1, tail, 0.0)
    return dv, dk, dg, dbeta


def local_kernel(q, k, v, do, s0, rows, dq, ub, w0, nb, tt, off, z, gram, gs, dk0, dg0):
    firsts = [local_first(q[i], k[i], v[i], s0[i], rows[i]) for i in range(q.shape[0])]
    invs = inverses([first[8] for first in firsts])
    for i in range(q.shape[0]):
        outs = local_rest(do[i], invs[i], firsts[i])
        for ref, value in zip((dq, ub, w0, nb, tt, off, z, gram, gs, dk0, dg0), outs):
            ref[i] = value.astype(ref.dtype)


def carry_kernel(k, v, s0, e, rows, ub, w0, nb, z, gram, gs, dk0, dg0, dv, dk, dg, dbeta):
    for i in range(k.shape[0]):
        outs = carry_head(
            k[i], v[i], s0[i], e[i], rows[i], ub[i], w0[i], nb[i], z[i], gram[i], gs[i], dk0[i], dg0[i]
        )
        for ref, value in zip((dv, dk, dg, dbeta), outs):
            ref[i] = value.astype(ref.dtype)


def chain_kernel(n, tt, off, rows, e_out, inbuf, outbuf, send_sem, recv_sem):
    me = lax.axis_index("seq")
    heads, c = tt.shape[0], rows.shape[2]
    barrier = pltpu.get_barrier_semaphore()
    mesh_id = pl.DeviceIdType.MESH

    @pl.when(me > 0)
    def _():
        pl.semaphore_signal(barrier, inc=1, device_id={"seq": me - 1}, device_id_type=mesh_id)

    @pl.when(me < n - 1)
    def _():
        pl.semaphore_signal(barrier, inc=1, device_id={"seq": me + 1}, device_id_type=mesh_id)

    peers = jnp.where(me > 0, 1, 0) + jnp.where(me < n - 1, 1, 0)
    pl.semaphore_wait(barrier, peers)

    def copy(h):
        return pltpu.make_async_remote_copy(
            src_ref=outbuf.at[h],
            dst_ref=inbuf.at[h],
            send_sem=send_sem.at[h],
            recv_sem=recv_sem.at[h],
            device_id={"seq": me - 1},
            device_id_type=mesh_id,
        )

    @pl.when(me == n - 1)
    def _():
        def first(h, _):
            outbuf[h] = off[h].astype(BF)
            copy(h).start()
            e_out[h] = jnp.zeros(e_out.shape[1:], e_out.dtype)
            return 0

        lax.fori_loop(0, heads, first, 0)

    @pl.when(me < n - 1)
    def _():
        def step(h, _):
            copy(h).wait_recv()
            e = inbuf[h]

            @pl.when(me > 0)
            def _():
                cdl = jnp.exp(rows[h, 0:1, c - 1 : c])
                outbuf[h] = (off[h] + cdl * e.astype(F32) - mm(tt[h], e)).astype(BF)
                copy(h).start()

            e_out[h] = e
            return 0

        lax.fori_loop(0, heads, step, 0)

    @pl.when(me > 0)
    def _():
        def done(h, _):
            copy(h).wait_send()
            return 0

        lax.fori_loop(0, heads, done, 0)


def sums_kernel(n, m, terms, halves, total, mine, got, part, gathered, got_half, sems, half_sems):
    me, side = lax.axis_index("seq"), lax.axis_index("head")
    mesh_id = pl.DeviceIdType.MESH
    barrier = pltpu.get_barrier_semaphore()

    def greet(d, _):
        pl.semaphore_signal(
            barrier, inc=1, device_id={"seq": lax.rem(me + d, n)}, device_id_type=mesh_id
        )
        return 0

    def greet_side(d, _):
        pl.semaphore_signal(
            barrier, inc=1, device_id={"head": lax.rem(side + d, m)}, device_id_type=mesh_id
        )
        return 0

    lax.fori_loop(1, n, greet, 0)
    lax.fori_loop(1, m, greet_side, 0)
    pl.semaphore_wait(barrier, n + m - 2)

    def scatter(to, source):
        return pltpu.make_async_remote_copy(
            src_ref=terms.at[to], dst_ref=got.at[source],
            send_sem=sems.at[0, to], recv_sem=sems.at[1, source],
            device_id={"seq": to}, device_id_type=mesh_id,
        )

    def gather(to, source):
        return pltpu.make_async_remote_copy(
            src_ref=part, dst_ref=gathered.at[source],
            send_sem=sems.at[2, to], recv_sem=sems.at[3, source],
            device_id={"seq": to}, device_id_type=mesh_id,
        )

    def swap(to, source):
        return pltpu.make_async_remote_copy(
            src_ref=halves.at[to], dst_ref=got_half.at[source],
            send_sem=half_sems.at[0, to], recv_sem=half_sems.at[1, source],
            device_id={"head": to}, device_id_type=mesh_id,
        )

    def ahead(d):
        return lax.rem(me + d, n)

    def behind(d):
        return lax.rem(me + n - d, n)

    def side_ahead(d):
        return lax.rem(side + d, m)

    def side_behind(d):
        return lax.rem(side + m - d, m)

    def run(count, body):
        def step(d, _):
            body(d)
            return 0

        lax.fori_loop(1, count, step, 0)

    run(n, lambda d: scatter(ahead(d), me).start())
    run(m, lambda d: swap(side_ahead(d), side).start())

    def add(d, acc):
        source = behind(d)
        scatter(source, source).wait_recv()
        return acc + got[source]

    acc = lax.fori_loop(1, n, add, terms[me])
    part[...] = acc
    total[me] = acc
    run(n, lambda d: gather(ahead(d), me).start())

    def add_half(d, acc):
        source = side_behind(d)
        swap(source, source).wait_recv()
        return acc + got_half[source].astype(F32)

    mine[...] = lax.fori_loop(1, m, add_half, halves[side].astype(F32)).astype(BF)

    def place(d):
        source = behind(d)
        gather(source, source).wait_recv()
        total[source] = gathered[source]

    run(n, place)
    run(n, lambda d: scatter(ahead(d), me).wait_send())
    run(n, lambda d: gather(ahead(d), me).wait_send())
    run(m, lambda d: swap(side_ahead(d), side).wait_send())


def sums_part(n, m, terms, halves):
    vm = pl.BlockSpec(memory_space=pltpu.VMEM)
    return pl.pallas_call(
        partial(sums_kernel, n, m),
        out_shape=(
            jax.ShapeDtypeStruct(terms.shape, F32),
            jax.ShapeDtypeStruct(halves.shape[1:], BF),
        ),
        in_specs=[vm] * 2,
        out_specs=(vm, vm),
        scratch_shapes=[
            pltpu.VMEM(terms.shape, F32),
            pltpu.VMEM(terms.shape[1:], F32),
            pltpu.VMEM(terms.shape, F32),
            pltpu.VMEM(halves.shape, BF),
            pltpu.SemaphoreType.DMA((4, n)),
            pltpu.SemaphoreType.DMA((2, m)),
        ],
        compiler_params=pltpu.CompilerParams(collective_id=1, has_side_effects=True),
    )(terms, halves)


def per_head(kernel, group, ins, outs):
    heads = ins[0].shape[0]

    def spec(a):
        return pl.BlockSpec((group,) + a.shape[1:], lambda h: (h, 0, 0))

    return pl.pallas_call(
        kernel,
        grid=(heads // group,),
        out_shape=outs,
        in_specs=[spec(a) for a in ins],
        out_specs=[spec(a) for a in outs],
        compiler_params=pltpu.CompilerParams(vmem_limit_bytes=48 * 1024 * 1024),
    )(*ins)


def local_part(q, k, v, do, s0, rows):
    h, c, dk = q.shape
    dv = v.shape[2]
    sd = jax.ShapeDtypeStruct
    outs = [
        sd((h, c, dk), BF), sd((h, c, dv), BF), sd((h, c, dv), F32), sd((h, c, dk), BF),
        sd((h, dk, dk), BF), sd((h, dk, dv), F32), sd((h, c, dv), F32), sd((h, c, c), F32),
        sd((h, c, c), F32), sd((h, c, dk), F32), sd((h, 1, c), F32),
    ]
    return per_head(local_kernel, 4, (q, k, v, do, s0, rows), outs)


def carry_part(k, v, s0, e, rows, saved):
    h, c, dk = k.shape
    dv = v.shape[2]
    sd = jax.ShapeDtypeStruct
    outs = [sd((h, c, dv), BF), sd((h, c, dk), BF), sd((h, 1, c), F32), sd((h, 1, c), F32)]
    return per_head(carry_kernel, 4, (k, v, s0, e, rows) + saved, outs)


def chain_part(n, tt, off, rows):
    vm = pl.BlockSpec(memory_space=pltpu.VMEM)
    h = tt.shape[0]
    return pl.pallas_call(
        partial(chain_kernel, n),
        out_shape=jax.ShapeDtypeStruct(off.shape, BF),
        in_specs=[vm] * 3,
        out_specs=vm,
        scratch_shapes=[
            pltpu.VMEM(off.shape, BF),
            pltpu.VMEM(off.shape, BF),
            pltpu.SemaphoreType.DMA((h,)),
            pltpu.SemaphoreType.DMA((h,)),
        ],
        compiler_params=pltpu.CompilerParams(collective_id=0, has_side_effects=True),
    )(tt, off, rows)


def gates(hidden_in, both, decay_bias, decay_log, write_bias):
    h = decay_bias.shape[0]
    logits = lax.dot_general(
        both, hidden_in, (((0,), (1,)), ((), ())), preferred_element_type=F32
    )
    pre = logits[:h] + decay_bias[:, None]
    rate = jnp.exp(decay_log)[:, None]
    beta = jax.nn.sigmoid(logits[h:] + write_bias[:, None])
    log_decay = -rate * jax.nn.softplus(pre)
    c = log_decay.shape[1]
    ones = jnp.triu(jnp.ones((c, c), F32))
    g = jnp.dot(log_decay, ones, precision=HI)
    return pre, rate, beta, g, ones


def shards(
    queries,
    key_vectors,
    values,
    out_grad,
    hidden_in,
    decay_weight,
    write_weight,
    decay_bias,
    decay_log,
    write_bias,
    start_state,
):
    n = lax.axis_size("seq")
    both = jnp.concatenate([decay_weight, write_weight], axis=1)
    pre, rate, beta, g, ones = gates(hidden_in, both, decay_bias, decay_log, write_bias)
    h, c = g.shape
    rows = jnp.concatenate(
        [g[:, None], beta[:, None], jnp.zeros((h, 6, c), F32)], axis=1
    )
    q, k, v, do = (jnp.swapaxes(a, 0, 1) for a in (queries, key_vectors, values, out_grad))
    s0 = start_state[0]
    dq, ub, w0, nb, tt, off, z, gram, gs, dk0, dg0 = local_part(q, k, v, do, s0, rows)
    e = chain_part(n, tt, off, rows)
    dv, dk, dg, dbeta = carry_part(k, v, s0, e, rows, (ub, w0, nb, z, gram, gs, dk0, dg0))
    dlog = jnp.dot(dg[:, 0], ones.T, precision=HI)
    decay_grads = (-dlog * rate * jax.nn.sigmoid(pre)).astype(BF)
    write_grads = (dbeta[:, 0] * beta * (1.0 - beta)).astype(BF)
    grads = jnp.concatenate([decay_grads, write_grads], axis=0)
    weight_terms = jnp.dot(grads, hidden_in, preferred_element_type=F32)
    width = hidden_in.shape[1]
    terms = jnp.swapaxes(weight_terms.reshape(2 * h, n, width // n), 0, 1)
    m = lax.axis_size("head")
    halves = lax.dot_general(
        jnp.broadcast_to(grads, (m,) + grads.shape),
        both.reshape(m, width // m, 2 * h),
        (((1,), (2,)), ((0,), (0,))),
        preferred_element_type=F32,
    ).astype(BF)
    total, grad_hidden = sums_part(n, m, terms, halves)
    total = jnp.swapaxes(total, 0, 1).reshape(2 * h, width)
    return (
        jnp.swapaxes(dq, 0, 1),
        jnp.swapaxes(dk, 0, 1),
        jnp.swapaxes(dv, 0, 1),
        grad_hidden,
        total[:h].T,
        total[h:].T,
    )


def solution(mesh):
    placed = (
        P("seq", "head", None),
        P("seq", "head", None),
        P("seq", "head", None),
        P("seq", "head", None),
        P("seq", None),
        P(None, "head"),
        P(None, "head"),
        P("head"),
        P("head"),
        P("head"),
        P("seq", "head", None, None),
    )
    return jax.shard_map(
        shards,
        mesh=mesh,
        in_specs=placed,
        out_specs=(
            P("seq", "head", None),
            P("seq", "head", None),
            P("seq", "head", None),
            P("seq", "head"),
            P(None, "head"),
            P(None, "head"),
        ),
        check_vma=False,
    )
```

```python
from functools import partial

import jax
import jax.numpy as jnp
from jax import lax
from jax.experimental import pallas as pl
from jax.experimental.pallas import tpu as pltpu
from jax.sharding import PartitionSpec as P

EPSILON = 1e-06
HI = lax.Precision.HIGHEST
F32 = jnp.float32
BF = jnp.bfloat16


def mm(a, b, ca=1, cb=0):
    return lax.dot_general(
        a.astype(BF), b.astype(BF), (((ca,), (cb,)), ((), ())), preferred_element_type=F32
    )


def unit(x):
    r = lax.rsqrt(jnp.sum(x * x, axis=1, keepdims=True) + EPSILON)
    return x * r, r


def unit_back(d, n, r):
    return r * (d - n * jnp.sum(n * d, axis=1, keepdims=True))


def indices(c):
    row = lax.broadcasted_iota(jnp.int32, (c, c), 0)
    col = lax.broadcasted_iota(jnp.int32, (c, c), 1)
    return row, col


def local_first(q, k, v, s0, rows):
    c = q.shape[0]
    row, col = indices(c)
    cols = rows.T
    g_col, beta = cols[:, 0:1], cols[:, 1:2]
    g_row = rows[0:1, :]
    g_last = g_row[:, c - 1 : c]
    cd = jnp.exp(g_col)
    to_end = jnp.exp(g_last - g_col)
    lower = row >= col
    gamma = jnp.where(lower, jnp.exp(jnp.where(lower, g_col - g_row, 0.0)), 0.0)
    gamma_strict = jnp.where(row > col, gamma, 0.0)
    qn, rq = unit(q.astype(F32))
    kn, _ = unit(k.astype(F32))
    qb, kb, sb = qn.astype(BF), kn.astype(BF), s0.astype(BF)
    gram = gamma_strict * mm(kb, kb, 1, 1)
    p = gamma * mm(qb, kb, 1, 1)
    z = v.astype(F32) - cd * mm(kb, sb)
    a = beta * gram
    return qn, rq, qb, kn, kb, sb, p, z, a, gram, gamma, gamma_strict, beta, cd, to_end


def inverses(couplings):
    c = couplings[0].shape[0]
    row, col = indices(c)
    invs = [
        jnp.where(row == col, 1.0, jnp.where((row ^ col) == 1, -a, 0.0)) for a in couplings
    ]
    level = 1
    while (2 << level) <= c:
        near = ((row >> level) ^ (col >> level)) == 1
        halves = [mm(x, jnp.where(near, a, 0.0)) for x, a in zip(invs, couplings)]
        invs = [x - mm(y, x) for x, y in zip(invs, halves)]
        level += 1
    return invs


def local_rest(do, inv, first):
    qn, rq, qb, kn, kb, sb, p, z, a, gram, gamma, gamma_strict, beta, cd, to_end = first
    ib = inv.astype(BF)
    ub = mm(ib, beta * z).astype(BF)
    ptdo = mm(p, do, 0, 0)
    w0 = mm(ib, ptdo, 0, 0)
    nb = mm(ib, to_end * kn, 0, 0).astype(BF)
    bck = ((beta * cd) * kn).astype(BF)
    off = mm(cd * qn, do, 0, 0) - mm(bck, w0, 0, 0)
    tt = mm(bck, nb, 0, 0)
    dp = mm(do, ub, 1, 1)
    dos = cd * mm(do, sb, 1, 1)
    gdp = (gamma * dp).astype(BF)
    dq = unit_back(dos + mm(gdp, kb), qn, rq)
    dk0 = mm(gdp, qb, 0, 0)
    t = dp * p
    dg0 = jnp.sum((t + dos * qn).T, axis=0, keepdims=True) - jnp.sum(t, axis=0, keepdims=True)
    return dq, ub, w0, nb, tt, off, z, gram, gamma_strict, dk0, dg0


def carry_head(k, v, s0, e, rows, ub, w0, nb, z, gram, gamma_strict, dk0, dg0):
    c = k.shape[0]
    row, col = indices(c)
    cols = rows.T
    g_col, beta = cols[:, 0:1], cols[:, 1:2]
    g_last = rows[0:1, c - 1 : c]
    cd = jnp.exp(g_col)
    to_end = jnp.exp(g_last - g_col)
    kn, rk = unit(k.astype(F32))
    kb = kn.astype(BF)
    w = w0 + mm(nb, e)
    wb = w.astype(BF)
    dv = beta * w
    da = -mm(wb, ub, 1, 1)
    ws = mm(wb, s0, 1, 1)
    ue = to_end * mm(ub, e, 1, 1)
    dkk = (beta * gamma_strict * da).astype(BF)
    dkn = dk0 - (beta * cd) * ws + mm(dkk, kb) + mm(dkk, kb, 0, 0) + ue
    dk = unit_back(dkn, kn, rk)
    dagram = da * gram
    t = beta * dagram
    s = kn * ue
    dbeta = jnp.sum((dagram + w * z).T, axis=0, keepdims=True)
    dg = dg0 - jnp.sum(t, axis=0, keepdims=True)
    dg = dg + jnp.sum((t - dv * (v.astype(F32) - z) - s).T, axis=0, keepdims=True)
    tail = jnp.sum(s, keepdims=True) + jnp.exp(g_last) * jnp.sum(s0 * e.astype(F32), keepdims=True)
    lane = lax.broadcasted_iota(jnp.int32, (1, c), 1)
    dg = dg + jnp.where(lane == c - 1, tail, 0.0)
    return dv, dk, dg, dbeta


def local_kernel(q, k, v, do, s0, rows, dq, ub, w0, nb, tt, off, z, gram, gs, dk0, dg0):
    firsts = [local_first(q[i], k[i], v[i], s0[i], rows[i]) for i in range(q.shape[0])]
    invs = inverses([first[8] for first in firsts])
    for i in range(q.shape[0]):
        outs = local_rest(do[i], invs[i], firsts[i])
        for ref, value in zip((dq, ub, w0, nb, tt, off, z, gram, gs, dk0, dg0), outs):
            ref[i] = value.astype(ref.dtype)


def carry_kernel(k, v, s0, e, rows, ub, w0, nb, z, gram, gs, dk0, dg0, dv, dk, dg, dbeta):
    for i in range(k.shape[0]):
        outs = carry_head(
            k[i], v[i], s0[i], e[i], rows[i], ub[i], w0[i], nb[i], z[i], gram[i], gs[i], dk0[i], dg0[i]
        )
        for ref, value in zip((dv, dk, dg, dbeta), outs):
            ref[i] = value.astype(ref.dtype)


def chain_kernel(n, tt, off, rows, e_out, inbuf, outbuf, send_sem, recv_sem):
    me = lax.axis_index("seq")
    heads, c = tt.shape[0], rows.shape[2]
    barrier = pltpu.get_barrier_semaphore()
    mesh_id = pl.DeviceIdType.MESH

    @pl.when(me > 0)
    def _():
        pl.semaphore_signal(barrier, inc=1, device_id={"seq": me - 1}, device_id_type=mesh_id)

    @pl.when(me < n - 1)
    def _():
        pl.semaphore_signal(barrier, inc=1, device_id={"seq": me + 1}, device_id_type=mesh_id)

    peers = jnp.where(me > 0, 1, 0) + jnp.where(me < n - 1, 1, 0)
    pl.semaphore_wait(barrier, peers)

    def copy(h):
        return pltpu.make_async_remote_copy(
            src_ref=outbuf.at[h],
            dst_ref=inbuf.at[h],
            send_sem=send_sem.at[h],
            recv_sem=recv_sem.at[h],
            device_id={"seq": me - 1},
            device_id_type=mesh_id,
        )

    @pl.when(me == n - 1)
    def _():
        def first(h, _):
            outbuf[h] = off[h].astype(BF)
            copy(h).start()
            e_out[h] = jnp.zeros(e_out.shape[1:], e_out.dtype)
            return 0

        lax.fori_loop(0, heads, first, 0)

    @pl.when(me < n - 1)
    def _():
        def step(h, _):
            copy(h).wait_recv()
            e = inbuf[h]

            @pl.when(me > 0)
            def _():
                cdl = jnp.exp(rows[h, 0:1, c - 1 : c])
                outbuf[h] = (off[h] + cdl * e.astype(F32) - mm(tt[h], e)).astype(BF)
                copy(h).start()

            e_out[h] = e
            return 0

        lax.fori_loop(0, heads, step, 0)

    @pl.when(me > 0)
    def _():
        def done(h, _):
            copy(h).wait_send()
            return 0

        lax.fori_loop(0, heads, done, 0)


def sums_kernel(n, m, terms, halves, total, mine, got, part, gathered, got_half, sems, half_sems):
    me, side = lax.axis_index("seq"), lax.axis_index("head")
    mesh_id = pl.DeviceIdType.MESH
    barrier = pltpu.get_barrier_semaphore()

    def greet(d, _):
        pl.semaphore_signal(
            barrier, inc=1, device_id={"seq": lax.rem(me + d, n)}, device_id_type=mesh_id
        )
        return 0

    def greet_side(d, _):
        pl.semaphore_signal(
            barrier, inc=1, device_id={"head": lax.rem(side + d, m)}, device_id_type=mesh_id
        )
        return 0

    lax.fori_loop(1, n, greet, 0)
    lax.fori_loop(1, m, greet_side, 0)
    pl.semaphore_wait(barrier, n + m - 2)

    def scatter(to, source):
        return pltpu.make_async_remote_copy(
            src_ref=terms.at[to], dst_ref=got.at[source],
            send_sem=sems.at[0, to], recv_sem=sems.at[1, source],
            device_id={"seq": to}, device_id_type=mesh_id,
        )

    def gather(to, source):
        return pltpu.make_async_remote_copy(
            src_ref=part, dst_ref=gathered.at[source],
            send_sem=sems.at[2, to], recv_sem=sems.at[3, source],
            device_id={"seq": to}, device_id_type=mesh_id,
        )

    def swap(to, source):
        return pltpu.make_async_remote_copy(
            src_ref=halves.at[to], dst_ref=got_half.at[source],
            send_sem=half_sems.at[0, to], recv_sem=half_sems.at[1, source],
            device_id={"head": to}, device_id_type=mesh_id,
        )

    def ahead(d):
        return lax.rem(me + d, n)

    def behind(d):
        return lax.rem(me + n - d, n)

    def side_ahead(d):
        return lax.rem(side + d, m)

    def side_behind(d):
        return lax.rem(side + m - d, m)

    def run(count, body):
        def step(d, _):
            body(d)
            return 0

        lax.fori_loop(1, count, step, 0)

    run(n, lambda d: scatter(ahead(d), me).start())
    run(m, lambda d: swap(side_ahead(d), side).start())

    def add(d, acc):
        source = behind(d)
        scatter(source, source).wait_recv()
        return acc + got[source]

    acc = lax.fori_loop(1, n, add, terms[me])
    part[...] = acc
    total[me] = acc
    run(n, lambda d: gather(ahead(d), me).start())

    def add_half(d, acc):
        source = side_behind(d)
        swap(source, source).wait_recv()
        return acc + got_half[source].astype(F32)

    mine[...] = lax.fori_loop(1, m, add_half, halves[side].astype(F32)).astype(BF)

    def place(d):
        source = behind(d)
        gather(source, source).wait_recv()
        total[source] = gathered[source]

    run(n, place)
    run(n, lambda d: scatter(ahead(d), me).wait_send())
    run(n, lambda d: gather(ahead(d), me).wait_send())
    run(m, lambda d: swap(side_ahead(d), side).wait_send())


def sums_part(n, m, terms, halves):
    vm = pl.BlockSpec(memory_space=pltpu.VMEM)
    return pl.pallas_call(
        partial(sums_kernel, n, m),
        out_shape=(
            jax.ShapeDtypeStruct(terms.shape, F32),
            jax.ShapeDtypeStruct(halves.shape[1:], BF),
        ),
        in_specs=[vm] * 2,
        out_specs=(vm, vm),
        scratch_shapes=[
            pltpu.VMEM(terms.shape, F32),
            pltpu.VMEM(terms.shape[1:], F32),
            pltpu.VMEM(terms.shape, F32),
            pltpu.VMEM(halves.shape, BF),
            pltpu.SemaphoreType.DMA((4, n)),
            pltpu.SemaphoreType.DMA((2, m)),
        ],
        compiler_params=pltpu.CompilerParams(collective_id=1, has_side_effects=True),
    )(terms, halves)


def per_head(kernel, group, ins, outs):
    heads = ins[0].shape[0]

    def spec(a):
        return pl.BlockSpec((group,) + a.shape[1:], lambda h: (h, 0, 0))

    return pl.pallas_call(
        kernel,
        grid=(heads // group,),
        out_shape=outs,
        in_specs=[spec(a) for a in ins],
        out_specs=[spec(a) for a in outs],
        compiler_params=pltpu.CompilerParams(vmem_limit_bytes=48 * 1024 * 1024),
    )(*ins)


def local_part(q, k, v, do, s0, rows):
    h, c, dk = q.shape
    dv = v.shape[2]
    sd = jax.ShapeDtypeStruct
    outs = [
        sd((h, c, dk), BF), sd((h, c, dv), BF), sd((h, c, dv), F32), sd((h, c, dk), BF),
        sd((h, dk, dk), BF), sd((h, dk, dv), F32), sd((h, c, dv), F32), sd((h, c, c), F32),
        sd((h, c, c), F32), sd((h, c, dk), F32), sd((h, 1, c), F32),
    ]
    return per_head(local_kernel, min(8, h), (q, k, v, do, s0, rows), outs)


def carry_part(k, v, s0, e, rows, saved):
    h, c, dk = k.shape
    dv = v.shape[2]
    sd = jax.ShapeDtypeStruct
    outs = [sd((h, c, dv), BF), sd((h, c, dk), BF), sd((h, 1, c), F32), sd((h, 1, c), F32)]
    return per_head(carry_kernel, 4, (k, v, s0, e, rows) + saved, outs)


def chain_part(n, tt, off, rows):
    vm = pl.BlockSpec(memory_space=pltpu.VMEM)
    h = tt.shape[0]
    return pl.pallas_call(
        partial(chain_kernel, n),
        out_shape=jax.ShapeDtypeStruct(off.shape, BF),
        in_specs=[vm] * 3,
        out_specs=vm,
        scratch_shapes=[
            pltpu.VMEM(off.shape, BF),
            pltpu.VMEM(off.shape, BF),
            pltpu.SemaphoreType.DMA((h,)),
            pltpu.SemaphoreType.DMA((h,)),
        ],
        compiler_params=pltpu.CompilerParams(collective_id=0, has_side_effects=True),
    )(tt, off, rows)


def gates(hidden_in, both, decay_bias, decay_log, write_bias):
    h = decay_bias.shape[0]
    logits = lax.dot_general(
        both, hidden_in, (((0,), (1,)), ((), ())), preferred_element_type=F32
    )
    pre = logits[:h] + decay_bias[:, None]
    rate = jnp.exp(decay_log)[:, None]
    beta = jax.nn.sigmoid(logits[h:] + write_bias[:, None])
    log_decay = -rate * jax.nn.softplus(pre)
    c = log_decay.shape[1]
    ones = jnp.triu(jnp.ones((c, c), F32))
    g = jnp.dot(log_decay, ones, precision=HI)
    return pre, rate, beta, g, ones


def shards(
    queries,
    key_vectors,
    values,
    out_grad,
    hidden_in,
    decay_weight,
    write_weight,
    decay_bias,
    decay_log,
    write_bias,
    start_state,
):
    n = lax.axis_size("seq")
    both = jnp.concatenate([decay_weight, write_weight], axis=1)
    pre, rate, beta, g, ones = gates(hidden_in, both, decay_bias, decay_log, write_bias)
    h, c = g.shape
    rows = jnp.concatenate(
        [g[:, None], beta[:, None], jnp.zeros((h, 6, c), F32)], axis=1
    )
    q, k, v, do = (jnp.swapaxes(a, 0, 1) for a in (queries, key_vectors, values, out_grad))
    s0 = start_state[0]
    dq, ub, w0, nb, tt, off, z, gram, gs, dk0, dg0 = local_part(q, k, v, do, s0, rows)
    e = chain_part(n, tt, off, rows)
    dv, dk, dg, dbeta = carry_part(k, v, s0, e, rows, (ub, w0, nb, z, gram, gs, dk0, dg0))
    dlog = jnp.dot(dg[:, 0], ones.T, precision=HI)
    decay_grads = (-dlog * rate * jax.nn.sigmoid(pre)).astype(BF)
    write_grads = (dbeta[:, 0] * beta * (1.0 - beta)).astype(BF)
    grads = jnp.concatenate([decay_grads, write_grads], axis=0)
    weight_terms = jnp.dot(grads, hidden_in, preferred_element_type=F32)
    width = hidden_in.shape[1]
    terms = jnp.swapaxes(weight_terms.reshape(2 * h, n, width // n), 0, 1)
    m = lax.axis_size("head")
    halves = lax.dot_general(
        jnp.broadcast_to(grads, (m,) + grads.shape),
        both.reshape(m, width // m, 2 * h),
        (((1,), (2,)), ((0,), (0,))),
        preferred_element_type=F32,
    ).astype(BF)
    total, grad_hidden = sums_part(n, m, terms, halves)
    total = jnp.swapaxes(total, 0, 1).reshape(2 * h, width)
    return (
        jnp.swapaxes(dq, 0, 1),
        jnp.swapaxes(dk, 0, 1),
        jnp.swapaxes(dv, 0, 1),
        grad_hidden,
        total[:h].T,
        total[h:].T,
    )


def solution(mesh):
    placed = (
        P("seq", "head", None),
        P("seq", "head", None),
        P("seq", "head", None),
        P("seq", "head", None),
        P("seq", None),
        P(None, "head"),
        P(None, "head"),
        P("head"),
        P("head"),
        P("head"),
        P("seq", "head", None, None),
    )
    return jax.shard_map(
        shards,
        mesh=mesh,
        in_specs=placed,
        out_specs=(
            P("seq", "head", None),
            P("seq", "head", None),
            P("seq", "head", None),
            P("seq", "head"),
            P(None, "head"),
            P(None, "head"),
        ),
        check_vma=False,
    )
```
